32 devices in a mesh: parts: 2 (over y), seq: 4 (over z), head: 4 (over x, core).
Axes of the slice: x: 2, y: 2, z: 4, core: 2. Of those that a mesh axis runs over, the one named last changes fastest.
Arguments:
- query_rows: bfloat16 [6144, 4096], P(('parts', 'seq', 'head')), parts along dimension 0, may hold values from -12 to 12
- key_rows: bfloat16 [6144, 4096], P(('parts', 'seq', 'head')), parts along dimension 0, may hold values from -12 to 12
- value_rows: bfloat16 [6144, 4096], P(('parts', 'seq', 'head')), parts along dimension 0, may hold values from -6 to 6
- block_lists: int32 [64, 4, 4, 3], P('parts', 'seq'), parts along dimension 0, may hold values from 0 to 5, as said below
- block_counts: int32 [64, 4, 4], P('parts'), parts along dimension 0, may hold values from 0 to 3, as said below
Outputs:
- attended: bfloat16 [6144, 4096], P(('parts', 'seq', 'head')), parts along dimension 0
The draws below stay inside these ranges and needn't reach their ends.
There are 2 independent parts, one for each index of `parts`. The reference program is written for one: setup_inputs(seed, part) draws one part's arguments, and reference() takes and returns one part's arrays. A program takes and returns all parts, laid end to end along the dimension named above; each array names one. Nothing has to cross between parts.
Inputs may be any that keep to these rules, and one draw needn't show every extreme that they name: `block_lists`: for one head, query tile and key tile the 3 entries are distinct block numbers of the key tile; only the first block_counts of them are listed. `block_counts`: 0 where the key tile is the query tile; some entries of every draw equal 3; for every k, query tile and key tile, the counts of heads 2k and 2k+1 sum to at most 4, and exactly 4 for some k in every draw.
All inputs are finite; a program needn't handle non-finite values.
Results may differ from the reference program's by a relative error of at most 0.0034.
Values may be sent and summed in bfloat16 or wider, within the bound.
A program may use at most 64 MiB of HBM per device.

```python
import math
import jax
import jax.numpy as jnp
from jax import lax

HEADS = 32
DH = 128
BLOCK = 128
MOST = 3
PAIR_MOST = 4
TILE = 768
TILES = 4
SEQ_LEN = 3072


def draw_query_rows(key, part):
    bulk = jnp.clip(1.75 * jax.random.normal(jax.random.fold_in(key, 41), (SEQ_LEN, HEADS * DH), jnp.float32), -12.0, 12.0)
    return bulk.astype(jnp.bfloat16)


def draw_key_rows(key, part):
    bulk = jnp.clip(1.75 * jax.random.normal(jax.random.fold_in(key, 43), (SEQ_LEN, HEADS * DH), jnp.float32), -12.0, 12.0)
    return bulk.astype(jnp.bfloat16)


def draw_block_lists(key, part):
    block_total = TILE // BLOCK
    scores = jax.random.randint(jax.random.fold_in(key, 21), (HEADS, TILES, TILES, block_total), 0, 1 << 20)
    scores = scores * block_total + jnp.arange(block_total, dtype=jnp.int32)
    return lax.top_k(scores, MOST)[1].astype(jnp.int32)


def draw_block_counts(key, part):
    pair_total = HEADS // 2
    density_level = jax.random.permutation(jax.random.fold_in(key, 31), pair_total) % 3
    busy_sum = jax.random.randint(jax.random.fold_in(key, 32), (pair_total, TILES, TILES), MOST, PAIR_MOST + 1)
    sparse_sum = jax.random.randint(jax.random.fold_in(key, 33), (pair_total, TILES, TILES), 0, 2)
    level_grid = density_level[:, None, None]
    pair_sum = jnp.where(level_grid == 2, PAIR_MOST, jnp.where(level_grid == 1, busy_sum, sparse_sum))
    lower_end = jnp.maximum(pair_sum - MOST, 0)
    upper_end = jnp.minimum(pair_sum, MOST)
    split_draw = jax.random.randint(jax.random.fold_in(key, 34), (pair_total, TILES, TILES), 0, 1 << 20)
    first_count = lower_end + split_draw % (upper_end - lower_end + 1)
    first_count = jnp.where(level_grid == 2, MOST, first_count)
    second_count = pair_sum - first_count
    counts_grid = jnp.stack([first_count, second_count], axis=1).reshape(HEADS, TILES, TILES)
    own_tile = jnp.arange(TILES)[:, None] == jnp.arange(TILES)[None, :]
    return jnp.where(own_tile[None], 0, counts_grid).astype(jnp.int32)


def steps_of(key, dims, split, least, high):
    level, own = 1.0, jax.random.fold_in(key, 6)
    for position, blocks in split:
        heights = jnp.exp(jax.random.uniform(jax.random.fold_in(own, position), (blocks,), jnp.float32, least / len(split), high / len(split)))
        level = level * jnp.repeat(heights, dims[position] // blocks).reshape([-1 if axis == position else 1 for axis in range(len(dims))])
    return level


def centred(stream_key, extent, deviation, bound, split=(), held_as=jnp.bfloat16):
    factor_of = steps_of(stream_key, extent, split, -0.22, 0.18) if split else 1.0
    values = jax.random.normal(stream_key, extent, jnp.float32) * deviation * factor_of
    return jnp.minimum(jnp.maximum(values, -bound), bound).astype(held_as)


def setup_inputs(seed: int = 0, part: int = 0) -> dict:
    seeds = jax.random.split(jax.random.key(seed), 6)
    part_splits = jax.random.split(jax.random.fold_in(seeds[5], part), 6)
    query_rows = draw_query_rows(jax.random.fold_in(jax.random.fold_in(seeds[5], part), 71), part)
    key_rows = draw_key_rows(jax.random.fold_in(jax.random.fold_in(seeds[5], part), 71), part)
    value_rows = centred(part_splits[2], (SEQ_LEN, HEADS * DH), 1.0, 6.0, ((0, 16),))
    block_lists = draw_block_lists(jax.random.fold_in(jax.random.fold_in(seeds[5], part), 71), part)
    block_counts = draw_block_counts(jax.random.fold_in(jax.random.fold_in(seeds[5], part), 71), part)
    return dict(query_rows=query_rows, key_rows=key_rows, value_rows=value_rows, block_lists=block_lists, block_counts=block_counts)


def reference(query_rows, key_rows, value_rows, block_lists, block_counts):
    block_total = TILE // BLOCK
    score_scale = 1.0 / math.sqrt(DH)

    def one_head(head_index):
        head_queries = lax.dynamic_slice_in_dim(query_rows, head_index * DH, DH, 1)
        head_keys = lax.dynamic_slice_in_dim(key_rows, head_index * DH, DH, 1)
        head_values = lax.dynamic_slice_in_dim(value_rows, head_index * DH, DH, 1)
        key_blocks = head_keys.reshape(TILES * block_total, BLOCK, DH)
        value_blocks = head_values.reshape(TILES * block_total, BLOCK, DH)

        def one_tile(tile_index):
            tile_queries = lax.dynamic_slice_in_dim(head_queries, tile_index * TILE, TILE, 0)
            own_keys = lax.dynamic_slice_in_dim(head_keys, tile_index * TILE, TILE, 0)
            own_values = lax.dynamic_slice_in_dim(head_values, tile_index * TILE, TILE, 0)
            tile_lists = block_lists[head_index, tile_index].astype(jnp.int32)
            tile_counts = block_counts[head_index, tile_index].astype(jnp.int32)
            picks = (jnp.arange(TILES, dtype=jnp.int32)[:, None] * block_total + tile_lists).reshape(-1)
            live_slots = (jnp.arange(MOST, dtype=jnp.int32)[None, :] < tile_counts[:, None]).reshape(-1)
            far_keys = key_blocks[picks].reshape(TILES * MOST * BLOCK, DH)
            far_values = value_blocks[picks].reshape(TILES * MOST * BLOCK, DH)
            all_keys = jnp.concatenate([own_keys, far_keys], axis=0)
            all_values = jnp.concatenate([own_values, far_values], axis=0)
            live_keys = jnp.concatenate([jnp.ones((TILE,), bool), jnp.repeat(live_slots, BLOCK)])
            scores = jnp.dot(tile_queries, all_keys.T, preferred_element_type=jnp.float32) * score_scale
            scores = jnp.where(live_keys[None, :], scores, -jnp.inf)
            row_top = lax.optimization_barrier(jnp.max(scores, axis=1, keepdims=True))
            weights = jnp.exp(scores - row_top)
            denominator = lax.optimization_barrier(jnp.sum(weights, axis=1, keepdims=True))
            mixture = jnp.dot(weights.astype(jnp.bfloat16), all_values, preferred_element_type=jnp.float32)
            return (mixture / denominator).astype(jnp.bfloat16)
        return lax.map(one_tile, jnp.arange(TILES, dtype=jnp.int32))
    head_outputs = lax.map(one_head, jnp.arange(HEADS, dtype=jnp.int32))
    head_outputs = head_outputs.reshape(HEADS, TILES * TILE, DH)
    return jnp.transpose(head_outputs, (1, 0, 2)).reshape(TILES * TILE, HEADS * DH)
```

```python
import functools
import math

import jax
import jax.numpy as jnp
from jax import lax
from jax.experimental import pallas as pl
from jax.experimental.pallas import tpu as pltpu
from jax.sharding import PartitionSpec as P

HEADS = 32
DH = 128
BLOCK = 128
MOST = 3
PAIR_MOST = 4
TILE = 768
MESH = pl.DeviceIdType.MESH


def contract_last(a, b):
    return lax.dot_general(a, b, (((1,), (1,)), ((), ())), preferred_element_type=jnp.float32)


def body(dims, lists_ref, counts_ref, q_ref, k_ref, v_ref, out_ref, *scratch):
    H, S, rows, heads, piece = dims
    pairs = heads // 2
    chips = H // 2
    kb, vb, qb = scratch[:pairs], scratch[pairs : 2 * pairs], scratch[2 * pairs : 3 * pairs]
    (ob, pk, fk, lbuf, lsm, x_send, x_recv, z_send, z_recv, l_send, l_recv, l_loc, o_send, o_recv) = (
        scratch[3 * pairs :]
    )
    me = lax.axis_index("head")
    tile = lax.axis_index("seq")

    def peer_of(i):
        chip = lax.rem(lax.div(me, 2) + 1 + lax.div(i, 2), chips)
        return chip * 2 + lax.rem(me + i + 1, 2)

    def source_of(i):
        chip = lax.rem(lax.div(me, 2) + 2 * chips - 1 - lax.div(i, 2), chips)
        return chip * 2 + lax.rem(me + i + 1, 2)

    def tile_after(d):
        return lax.rem(tile + d, S)

    def i32(i):
        return jnp.int32(i)

    barrier = pltpu.get_barrier_semaphore()
    for i in range(H - 1):
        pl.semaphore_signal(barrier, inc=1, device_id={"head": peer_of(i32(i))}, device_id_type=MESH)
    for d in range(1, S):
        pl.semaphore_signal(barrier, inc=1, device_id={"seq": tile_after(d)}, device_id_type=MESH)

    sources = (k_ref, v_ref, q_ref)
    places = (kb, vb, qb)

    def pair_columns(owner, p):
        return pl.ds(pl.multiple_of((owner * heads + 2 * p) * DH, 2 * DH), 2 * DH)

    def row_range(owner):
        return pl.ds(pl.multiple_of(owner * rows, 16), rows)

    def source_at(a, owner, p):
        columns = pair_columns(owner, p)
        return sources[a].at[:, columns] if a == 2 else sources[a].at[:, :, columns]

    def place_at(a, owner, p):
        if a == 2:
            return places[a][p].at[row_range(owner), :]
        return places[a][p].at[pl.ds(owner * (rows // piece), rows // piece)]

    def own_copy(a, p):
        return pltpu.make_async_copy(
            source_at(a, me, p),
            place_at(a, me, p),
            x_recv.at[a, p, H - 1],
        )

    def x_copy(a, p, i, landed):
        to = peer_of(i32(i))
        at = source_of(i32(i)) if landed else me
        return pltpu.make_async_remote_copy(
            src_ref=source_at(a, to, p),
            dst_ref=place_at(a, at, p),
            send_sem=x_send.at[a, p, i],
            recv_sem=x_recv.at[a, p, i],
            device_id={"head": to},
            device_id_type=MESH,
        )

    def l_copy(d):
        to = tile_after(d)
        return pltpu.make_async_remote_copy(
            src_ref=lists_ref.at[to],
            dst_ref=lbuf.at[d - 1],
            send_sem=l_send.at[d - 1],
            recv_sem=l_recv.at[d - 1],
            device_id={"seq": to},
            device_id_type=MESH,
        )

    def z_copy(p, d):
        return pltpu.make_async_remote_copy(
            src_ref=pk.at[p, d - 1],
            dst_ref=fk.at[p, d - 1],
            send_sem=z_send.at[p, d - 1],
            recv_sem=z_recv.at[p, d - 1],
            device_id={"seq": tile_after(d)},
            device_id_type=MESH,
        )

    def o_copy(p, i, landed):
        to = peer_of(i)
        at = source_of(i) if landed else me
        return pltpu.make_async_remote_copy(
            src_ref=ob.at[p, i],
            dst_ref=out_ref.at[:, pair_columns(at, p)],
            send_sem=o_send.at[p, i],
            recv_sem=o_recv.at[p, i],
            device_id={"head": to},
            device_id_type=MESH,
        )

    def o_own(p):
        return pltpu.make_async_copy(
            ob.at[p, H - 1], out_ref.at[:, pair_columns(me, p)], o_recv.at[p, H - 1]
        )

    for p in range(pairs):
        for a in (0, 1):
            own_copy(a, p).start()
    for p in range(pairs):
        own_copy(2, p).start()
    pl.semaphore_wait(barrier, H - 1 + S - 1)
    for d in range(1, S):
        l_copy(d).start()
    for p in range(pairs):
        for a in (0, 1):
            for i in range(H - 1):
                x_copy(a, p, i, False).start()
    for p in range(pairs):
        for i in range(H - 1):
            x_copy(2, p, i, False).start()

    for d in range(1, S):
        l_copy(d).wait_recv()
    to_scalars = pltpu.make_async_copy(lbuf, lsm, l_loc)
    to_scalars.start()
    to_scalars.wait()

    def arrived(a, p):
        own_copy(a, p).wait()
        for i in range(H - 1):
            x_copy(a, p, i, True).wait_recv()

    def count_of(head_slot, query_tile, key_tile):
        return counts_ref[((me * heads + head_slot) * S + query_tile) * S + key_tile]

    for p in range(pairs):
        arrived(0, p)
        arrived(1, p)
        for d in range(1, S):
            first = count_of(2 * p, tile_after(d), tile)
            for s in range(PAIR_MOST):
                left = lsm[S - d - 1, 0, 2 * p * MOST + min(s, MOST - 1)]
                right = lsm[S - d - 1, 0, (2 * p + 1) * MOST + min(PAIR_MOST - 1 - s, MOST - 1)]
                for b in range(BLOCK // piece):
                    at = pl.ds(b * piece, piece)
                    for c, held in enumerate((kb[p], vb[p])):
                        if s < PAIR_MOST - 1:
                            chosen = held[left * (BLOCK // piece) + b, :, :DH]
                        if s > 0:
                            other = held[right * (BLOCK // piece) + b, :, DH:]
                            if s < PAIR_MOST - 1:
                                chosen = jnp.where(s < first, chosen, other)
                            else:
                                chosen = other
                        pk[p, d - 1, c, s, at, :] = chosen
            z_copy(p, d).start()

    factor = math.log2(math.e) / math.sqrt(DH)
    width = MOST * BLOCK
    lane = lax.broadcasted_iota(jnp.int32, (1, width), 1)
    for p in range(pairs):
        arrived(2, p)
        for d in range(1, S):
            z_copy(p, d).wait_recv()

        def chunk(i, carry, p=p):
            mine = row_range(peer_of(i))
            for hs in range(2):
                cols = slice(hs * DH, (hs + 1) * DH)
                q = qb[p][mine, cols]
                scores = [contract_last(q, kb[p][:, :, cols].reshape(TILE, DH))]
                values = [vb[p][:, :, cols].reshape(TILE, DH)]
                for d in range(1, S):
                    used = count_of(2 * p + hs, tile, lax.rem(tile + S - d, S)) * BLOCK
                    live = lane < used if hs == 0 else lane >= width - used
                    bias = jnp.where(live, 0.0, -jnp.inf).astype(jnp.float32)
                    far = fk[p, d - 1, 0, hs : hs + MOST].reshape(width, DH)
                    scores.append(contract_last(q, far) + bias)
                    values.append(fk[p, d - 1, 1, hs : hs + MOST].reshape(width, DH))
                top = functools.reduce(
                    jnp.maximum, [jnp.max(s, axis=1, keepdims=True) for s in scores]
                )
                total = jnp.zeros((rows, 1), jnp.float32)
                mixed = jnp.zeros((rows, DH), jnp.float32)
                for s, v in zip(scores, values):
                    w = jnp.exp2((s - top) * factor)
                    total = total + jnp.sum(w, axis=1, keepdims=True)
                    mixed = mixed + jnp.dot(
                        w.astype(jnp.bfloat16), v, preferred_element_type=jnp.float32
                    )
                ob[p, i, :, cols] = (mixed / total).astype(jnp.bfloat16)

            @pl.when(i < H - 1)
            def _():
                o_copy(p, i, False).start()

            return carry

        lax.fori_loop(0, H, chunk, 0)
        o_own(p).start()

    for p in range(pairs):
        o_own(p).wait()
        for i in range(H - 1):
            o_copy(p, i32(i), True).wait_recv()
    for d in range(1, S):
        l_copy(d).wait_send()
        for p in range(pairs):
            z_copy(p, d).wait_send()
    for p in range(pairs):
        for i in range(H - 1):
            for a in range(3):
                x_copy(a, p, i, False).wait_send()
            o_copy(p, i32(i), False).wait_send()


def on_device(query_rows, key_rows, value_rows, block_lists, block_counts):
    H = lax.axis_size("head")
    S = lax.axis_size("seq")
    me = lax.axis_index("head")
    rows = query_rows.shape[0]
    heads = HEADS // H
    pairs = heads // 2
    mine = lax.dynamic_slice_in_dim(block_lists[:, 0], me * heads, heads)
    lists = jnp.transpose(mine, (1, 0, 2)).reshape(S, 1, heads * MOST)
    lists = jnp.pad(lists, ((0, 0), (0, 0), (0, 128 - heads * MOST)))
    bf16 = jnp.bfloat16
    piece = math.gcd(rows, BLOCK)
    pieces = (rows // piece, piece, query_rows.shape[1])
    tile_buffers = [
        pltpu.VMEM((TILE // piece, piece, 2 * DH), bf16) for _ in range(2 * pairs)
    ] + [pltpu.VMEM((TILE, 2 * DH), bf16) for _ in range(pairs)]
    anywhere = pl.BlockSpec(memory_space=pl.ANY)
    return pl.pallas_call(
        functools.partial(body, (H, S, rows, heads, piece)),
        out_shape=jax.ShapeDtypeStruct(query_rows.shape, bf16),
        in_specs=[anywhere, pl.BlockSpec(memory_space=pltpu.SMEM), anywhere, anywhere, anywhere],
        out_specs=anywhere,
        scratch_shapes=tile_buffers
        + [
            pltpu.VMEM((pairs, H, rows, 2 * DH), bf16),
            pltpu.VMEM((pairs, S - 1, 2, PAIR_MOST, BLOCK, DH), bf16),
            pltpu.VMEM((pairs, S - 1, 2, PAIR_MOST, BLOCK, DH), bf16),
            pltpu.VMEM((S - 1, 1, 128), jnp.int32),
            pltpu.SMEM((S - 1, 1, 128), jnp.int32),
            pltpu.SemaphoreType.DMA((3, pairs, H)),
            pltpu.SemaphoreType.DMA((3, pairs, H)),
            pltpu.SemaphoreType.DMA((pairs, S - 1)),
            pltpu.SemaphoreType.DMA((pairs, S - 1)),
            pltpu.SemaphoreType.DMA((S - 1,)),
            pltpu.SemaphoreType.DMA((S - 1,)),
            pltpu.SemaphoreType.DMA,
            pltpu.SemaphoreType.DMA((pairs, H)),
            pltpu.SemaphoreType.DMA((pairs, H)),
        ],
        compiler_params=pltpu.CompilerParams(
            collective_id=0, has_side_effects=True, vmem_limit_bytes=60 << 20
        ),
        name="block_attention",
    )(lists, block_counts.reshape(-1), query_rows, key_rows.reshape(pieces), value_rows.reshape(pieces))


def solution(mesh):
    in_specs = (
        P(("parts", "seq", "head"), None),
        P(("parts", "seq", "head"), None),
        P(("parts", "seq", "head"), None),
        P("parts", "seq", None, None),
        P("parts", None, None),
    )
    out_specs = P(("parts", "seq", "head"), None)
    return jax.shard_map(
        on_device, mesh=mesh, in_specs=in_specs, out_specs=out_specs, check_vma=False
    )
```

```python
import functools
import math

import jax
import jax.numpy as jnp
from jax import lax
from jax.experimental import pallas as pl
from jax.experimental.pallas import tpu as pltpu
from jax.sharding import PartitionSpec as P

HEADS = 32
DH = 128
BLOCK = 128
MOST = 3
PAIR_MOST = 4
TILE = 768
MESH = pl.DeviceIdType.MESH


def contract_last(a, b):
    return lax.dot_general(a, b, (((1,), (1,)), ((), ())), preferred_element_type=jnp.float32)


def body(dims, lists_ref, counts_ref, q_ref, k_ref, v_ref, out_ref, *scratch):
    H, S, rows, heads, piece = dims
    pairs = heads // 2
    chips = H // 2
    kb, vb, qb = scratch[:pairs], scratch[pairs : 2 * pairs], scratch[2 * pairs : 3 * pairs]
    (ob, pk, fk, lbuf, lsm, x_send, x_recv, z_send, z_recv, l_send, l_recv, l_loc, o_send, o_recv) = (
        scratch[3 * pairs :]
    )
    me = lax.axis_index("head")
    tile = lax.axis_index("seq")

    def peer_of(i):
        chip = lax.rem(lax.div(me, 2) + 1 + lax.div(i, 2), chips)
        return chip * 2 + lax.rem(me + i + 1, 2)

    def source_of(i):
        chip = lax.rem(lax.div(me, 2) + 2 * chips - 1 - lax.div(i, 2), chips)
        return chip * 2 + lax.rem(me + i + 1, 2)

    def tile_after(d):
        return lax.rem(tile + d, S)

    def i32(i):
        return jnp.int32(i)

    barrier = pltpu.get_barrier_semaphore()
    for i in range(H - 1):
        pl.semaphore_signal(barrier, inc=1, device_id={"head": peer_of(i32(i))}, device_id_type=MESH)
    for d in range(1, S):
        pl.semaphore_signal(barrier, inc=1, device_id={"seq": tile_after(d)}, device_id_type=MESH)

    sources = (k_ref, v_ref, q_ref)
    places = (kb, vb, qb)

    def pair_columns(owner, p):
        return pl.ds(pl.multiple_of((owner * heads + 2 * p) * DH, 2 * DH), 2 * DH)

    def row_range(owner):
        return pl.ds(pl.multiple_of(owner * rows, 16), rows)

    def source_at(a, owner, p):
        columns = pair_columns(owner, p)
        return sources[a].at[:, columns] if a == 2 else sources[a].at[:, :, columns]

    def place_at(a, owner, p):
        if a == 2:
            return places[a][p].at[row_range(owner), :]
        return places[a][p].at[pl.ds(owner * (rows // piece), rows // piece)]

    def own_copy(a, p):
        return pltpu.make_async_copy(
            source_at(a, me, p),
            place_at(a, me, p),
            x_recv.at[a, p, H - 1],
        )

    def x_copy(a, p, i, landed):
        to = peer_of(i32(i))
        at = source_of(i32(i)) if landed else me
        return pltpu.make_async_remote_copy(
            src_ref=source_at(a, to, p),
            dst_ref=place_at(a, at, p),
            send_sem=x_send.at[a, p, i],
            recv_sem=x_recv.at[a, p, i],
            device_id={"head": to},
            device_id_type=MESH,
        )

    def l_copy(d):
        to = tile_after(d)
        return pltpu.make_async_remote_copy(
            src_ref=lists_ref.at[to],
            dst_ref=lbuf.at[d - 1],
            send_sem=l_send.at[d - 1],
            recv_sem=l_recv.at[d - 1],
            device_id={"seq": to},
            device_id_type=MESH,
        )

    def z_copy(p, d, c):
        return pltpu.make_async_remote_copy(
            src_ref=pk.at[p, d - 1, c],
            dst_ref=fk.at[p, d - 1, c],
            send_sem=z_send.at[p, d - 1, c],
            recv_sem=z_recv.at[p, d - 1, c],
            device_id={"seq": tile_after(d)},
            device_id_type=MESH,
        )

    def o_copy(p, i, landed):
        to = peer_of(i)
        at = source_of(i) if landed else me
        return pltpu.make_async_remote_copy(
            src_ref=ob.at[p, i],
            dst_ref=out_ref.at[:, pair_columns(at, p)],
            send_sem=o_send.at[p, i],
            recv_sem=o_recv.at[p, i],
            device_id={"head": to},
            device_id_type=MESH,
        )

    def o_own(p):
        return pltpu.make_async_copy(
            ob.at[p, H - 1], out_ref.at[:, pair_columns(me, p)], o_recv.at[p, H - 1]
        )

    pl.semaphore_wait(barrier, H - 1 + S - 1)
    for d in range(1, S):
        l_copy(d).start()
    for p in range(pairs):
        for a in (0, 1):
            for i in range(H - 1):
                x_copy(a, p, i, False).start()
            own_copy(a, p).start()
    for p in range(pairs):
        for i in range(H - 1):
            x_copy(2, p, i, False).start()
        own_copy(2, p).start()

    for d in range(1, S):
        l_copy(d).wait_recv()
    to_scalars = pltpu.make_async_copy(lbuf, lsm, l_loc)
    to_scalars.start()
    to_scalars.wait()

    def arrived(a, p):
        own_copy(a, p).wait()
        for i in range(H - 1):
            x_copy(a, p, i, True).wait_recv()

    def count_of(head_slot, query_tile, key_tile):
        return counts_ref[((me * heads + head_slot) * S + query_tile) * S + key_tile]

    for p in range(pairs):
        for c, held in enumerate((kb[p], vb[p])):
            arrived(c, p)
            for d in range(1, S):
                first = count_of(2 * p, tile_after(d), tile)
                for s in range(PAIR_MOST):
                    left = lsm[S - d - 1, 0, 2 * p * MOST + min(s, MOST - 1)]
                    right = lsm[S - d - 1, 0, (2 * p + 1) * MOST + min(PAIR_MOST - 1 - s, MOST - 1)]
                    for b in range(BLOCK // piece):
                        if s < PAIR_MOST - 1:
                            chosen = held[left * (BLOCK // piece) + b, :, :DH]
                        if s > 0:
                            other = held[right * (BLOCK // piece) + b, :, DH:]
                            if s < PAIR_MOST - 1:
                                chosen = jnp.where(s < first, chosen, other)
                            else:
                                chosen = other
                        pk[p, d - 1, c, s, pl.ds(b * piece, piece), :] = chosen
                z_copy(p, d, c).start()

    factor = math.log2(math.e) / math.sqrt(DH)
    width = MOST * BLOCK
    lane = lax.broadcasted_iota(jnp.int32, (1, width), 1)
    for p in range(pairs):
        arrived(2, p)
        for d in range(1, S):
            for c in range(2):
                z_copy(p, d, c).wait_recv()

        def chunk(i, carry, p=p):
            mine = row_range(peer_of(i))
            for hs in range(2):
                cols = slice(hs * DH, (hs + 1) * DH)
                q = qb[p][mine, cols]
                scores = [contract_last(q, kb[p][:, :, cols].reshape(TILE, DH))]
                values = [vb[p][:, :, cols].reshape(TILE, DH)]
                for d in range(1, S):
                    used = count_of(2 * p + hs, tile, lax.rem(tile + S - d, S)) * BLOCK
                    live = lane < used if hs == 0 else lane >= width - used
                    bias = jnp.where(live, 0.0, -jnp.inf).astype(jnp.float32)
                    far = fk[p, d - 1, 0, hs : hs + MOST].reshape(width, DH)
                    scores.append(contract_last(q, far) + bias)
                    values.append(fk[p, d - 1, 1, hs : hs + MOST].reshape(width, DH))
                top = functools.reduce(
                    jnp.maximum, [jnp.max(s, axis=1, keepdims=True) for s in scores]
                )
                total = jnp.zeros((rows, 1), jnp.float32)
                mixed = jnp.zeros((rows, DH), jnp.float32)
                for s, v in zip(scores, values):
                    w = jnp.exp2((s - top) * factor)
                    total = total + jnp.sum(w, axis=1, keepdims=True)
                    mixed = mixed + jnp.dot(
                        w.astype(jnp.bfloat16), v, preferred_element_type=jnp.float32
                    )
                ob[p, i, :, cols] = (mixed / total).astype(jnp.bfloat16)

            @pl.when(i < H - 1)
            def _():
                o_copy(p, i, False).start()

            return carry

        lax.fori_loop(0, H, chunk, 0)
        o_own(p).start()

    for p in range(pairs):
        o_own(p).wait()
        for i in range(H - 1):
            o_copy(p, i32(i), True).wait_recv()
    for d in range(1, S):
        l_copy(d).wait_send()
        for p in range(pairs):
            for c in range(2):
                z_copy(p, d, c).wait_send()
    for p in range(pairs):
        for i in range(H - 1):
            for a in range(3):
                x_copy(a, p, i, False).wait_send()
            o_copy(p, i32(i), False).wait_send()


def on_device(query_rows, key_rows, value_rows, block_lists, block_counts):
    H = lax.axis_size("head")
    S = lax.axis_size("seq")
    me = lax.axis_index("head")
    rows = query_rows.shape[0]
    heads = HEADS // H
    pairs = heads // 2
    mine = lax.dynamic_slice_in_dim(block_lists[:, 0], me * heads, heads)
    lists = jnp.transpose(mine, (1, 0, 2)).reshape(S, 1, heads * MOST)
    lists = jnp.pad(lists, ((0, 0), (0, 0), (0, 128 - heads * MOST)))
    bf16 = jnp.bfloat16
    piece = math.gcd(rows, BLOCK)
    pieces = (rows // piece, piece, query_rows.shape[1])
    tile_buffers = [
        pltpu.VMEM((TILE // piece, piece, 2 * DH), bf16) for _ in range(2 * pairs)
    ] + [pltpu.VMEM((TILE, 2 * DH), bf16) for _ in range(pairs)]
    anywhere = pl.BlockSpec(memory_space=pl.ANY)
    return pl.pallas_call(
        functools.partial(body, (H, S, rows, heads, piece)),
        out_shape=jax.ShapeDtypeStruct(query_rows.shape, bf16),
        in_specs=[anywhere, pl.BlockSpec(memory_space=pltpu.SMEM), anywhere, anywhere, anywhere],
        out_specs=anywhere,
        scratch_shapes=tile_buffers
        + [
            pltpu.VMEM((pairs, H, rows, 2 * DH), bf16),
            pltpu.VMEM((pairs, S - 1, 2, PAIR_MOST, BLOCK, DH), bf16),
            pltpu.VMEM((pairs, S - 1, 2, PAIR_MOST, BLOCK, DH), bf16),
            pltpu.VMEM((S - 1, 1, 128), jnp.int32),
            pltpu.SMEM((S - 1, 1, 128), jnp.int32),
            pltpu.SemaphoreType.DMA((3, pairs, H)),
            pltpu.SemaphoreType.DMA((3, pairs, H)),
            pltpu.SemaphoreType.DMA((pairs, S - 1, 2)),
            pltpu.SemaphoreType.DMA((pairs, S - 1, 2)),
            pltpu.SemaphoreType.DMA((S - 1,)),
            pltpu.SemaphoreType.DMA((S - 1,)),
            pltpu.SemaphoreType.DMA,
            pltpu.SemaphoreType.DMA((pairs, H)),
            pltpu.SemaphoreType.DMA((pairs, H)),
        ],
        compiler_params=pltpu.CompilerParams(
            collective_id=0, has_side_effects=True, vmem_limit_bytes=60 << 20
        ),
        name="block_attention",
    )(lists, block_counts.reshape(-1), query_rows, key_rows.reshape(pieces), value_rows.reshape(pieces))


def solution(mesh):
    in_specs = (
        P(("parts", "seq", "head"), None),
        P(("parts", "seq", "head"), None),
        P(("parts", "seq", "head"), None),
        P("parts", "seq", None, None),
        P("parts", None, None),
    )
    out_specs = P(("parts", "seq", "head"), None)
    return jax.shard_map(
        on_device, mesh=mesh, in_specs=in_specs, out_specs=out_specs, check_vma=False
    )
```

```python
import functools
import math

import jax
import jax.numpy as jnp
from jax import lax
from jax.experimental import pallas as pl
from jax.experimental.pallas import tpu as pltpu
from jax.sharding import PartitionSpec as P

HEADS = 32
DH = 128
BLOCK = 128
MOST = 3
PAIR_MOST = 4
TILE = 768
MESH = pl.DeviceIdType.MESH


def contract_last(a, b):
    return lax.dot_general(a, b, (((1,), (1,)), ((), ())), preferred_element_type=jnp.float32)


def body(dims, lists_ref, q_ref, k_ref, v_ref, out_ref, *scratch):
    H, S, rows, heads, piece = dims
    pairs = heads // 2
    chips = H // 2
    kb, vb, qb = scratch[:pairs], scratch[pairs : 2 * pairs], scratch[2 * pairs : 3 * pairs]
    (ob, pk, fk, lbuf, lsm, own_lists, x_send, x_recv, z_send, z_recv, l_send, l_recv, l_loc, o_send, o_recv) = (
        scratch[3 * pairs :]
    )
    me = lax.axis_index("head")
    tile = lax.axis_index("seq")

    def peer_of(i):
        chip = lax.rem(lax.div(me, 2) + 1 + lax.div(i, 2), chips)
        return chip * 2 + lax.rem(me + i + 1, 2)

    def source_of(i):
        chip = lax.rem(lax.div(me, 2) + 2 * chips - 1 - lax.div(i, 2), chips)
        return chip * 2 + lax.rem(me + i + 1, 2)

    def tile_after(d):
        return lax.rem(tile + d, S)

    def i32(i):
        return jnp.int32(i)

    barrier = pltpu.get_barrier_semaphore()
    for i in range(H - 1):
        pl.semaphore_signal(barrier, inc=1, device_id={"head": peer_of(i32(i))}, device_id_type=MESH)
    for d in range(1, S):
        pl.semaphore_signal(barrier, inc=1, device_id={"seq": tile_after(d)}, device_id_type=MESH)

    sources = (k_ref, v_ref, q_ref)
    places = (kb, vb, qb)

    def pair_columns(owner, p):
        return pl.ds(pl.multiple_of((owner * heads + 2 * p) * DH, 2 * DH), 2 * DH)

    def row_range(owner):
        return pl.ds(pl.multiple_of(owner * rows, 16), rows)

    def source_at(a, owner, p):
        columns = pair_columns(owner, p)
        return sources[a].at[:, columns] if a == 2 else sources[a].at[:, :, columns]

    def place_at(a, owner, p):
        if a == 2:
            return places[a][p].at[row_range(owner), :]
        return places[a][p].at[pl.ds(owner * (rows // piece), rows // piece)]

    def own_copy(a, p):
        return pltpu.make_async_copy(
            source_at(a, me, p),
            place_at(a, me, p),
            x_recv.at[a, p, H - 1],
        )

    def x_copy(a, p, i, landed):
        to = peer_of(i32(i))
        at = source_of(i32(i)) if landed else me
        return pltpu.make_async_remote_copy(
            src_ref=source_at(a, to, p),
            dst_ref=place_at(a, at, p),
            send_sem=x_send.at[a, p, i],
            recv_sem=x_recv.at[a, p, i],
            device_id={"head": to},
            device_id_type=MESH,
        )

    def l_copy(d):
        to = tile_after(d)
        return pltpu.make_async_remote_copy(
            src_ref=lists_ref.at[to],
            dst_ref=lbuf.at[d - 1],
            send_sem=l_send.at[d - 1],
            recv_sem=l_recv.at[d - 1],
            device_id={"seq": to},
            device_id_type=MESH,
        )

    def z_copy(p, d, c):
        return pltpu.make_async_remote_copy(
            src_ref=pk.at[p, d - 1, c],
            dst_ref=fk.at[p, d - 1, c],
            send_sem=z_send.at[p, d - 1, c],
            recv_sem=z_recv.at[p, d - 1, c],
            device_id={"seq": tile_after(d)},
            device_id_type=MESH,
        )

    def o_copy(p, i, landed):
        to = peer_of(i)
        at = source_of(i) if landed else me
        return pltpu.make_async_remote_copy(
            src_ref=ob.at[p, i],
            dst_ref=out_ref.at[:, pair_columns(at, p)],
            send_sem=o_send.at[p, i],
            recv_sem=o_recv.at[p, i],
            device_id={"head": to},
            device_id_type=MESH,
        )

    def o_own(p):
        return pltpu.make_async_copy(
            ob.at[p, H - 1], out_ref.at[:, pair_columns(me, p)], o_recv.at[p, H - 1]
        )

    own_scalars = pltpu.make_async_copy(lists_ref, own_lists, l_loc.at[1])
    own_scalars.start()
    pl.semaphore_wait(barrier, H - 1 + S - 1)
    for d in range(1, S):
        l_copy(d).start()
    for p in range(pairs):
        for a in (0, 1):
            for i in range(H - 1):
                x_copy(a, p, i, False).start()
            own_copy(a, p).start()
    for p in range(pairs):
        for i in range(H - 1):
            x_copy(2, p, i, False).start()
        own_copy(2, p).start()

    for d in range(1, S):
        l_copy(d).wait_recv()
    to_scalars = pltpu.make_async_copy(lbuf, lsm, l_loc.at[0])
    to_scalars.start()
    to_scalars.wait()

    def arrived(a, p):
        own_copy(a, p).wait()
        for i in range(H - 1):
            x_copy(a, p, i, True).wait_recv()

    own_scalars.wait()

    def count_of(head_slot, query_tile, key_tile):
        return own_lists[key_tile, 0, heads * MOST + head_slot]

    for p in range(pairs):
        for c, held in enumerate((kb[p], vb[p])):
            arrived(c, p)
            for d in range(1, S):
                first = lsm[S - d - 1, 0, heads * MOST + 2 * p]
                for s in range(PAIR_MOST):
                    left = lsm[S - d - 1, 0, 2 * p * MOST + min(s, MOST - 1)]
                    right = lsm[S - d - 1, 0, (2 * p + 1) * MOST + min(PAIR_MOST - 1 - s, MOST - 1)]
                    for b in range(BLOCK // piece):
                        if s < PAIR_MOST - 1:
                            chosen = held[left * (BLOCK // piece) + b, :, :DH]
                        if s > 0:
                            other = held[right * (BLOCK // piece) + b, :, DH:]
                            if s < PAIR_MOST - 1:
                                chosen = jnp.where(s < first, chosen, other)
                            else:
                                chosen = other
                        pk[p, d - 1, c, s, pl.ds(b * piece, piece), :] = chosen
                z_copy(p, d, c).start()

    factor = math.log2(math.e) / math.sqrt(DH)
    width = MOST * BLOCK
    lane = lax.broadcasted_iota(jnp.int32, (1, width), 1)
    for p in range(pairs):
        arrived(2, p)
        for d in range(1, S):
            for c in range(2):
                z_copy(p, d, c).wait_recv()

        def chunk(i, carry, p=p):
            mine = row_range(peer_of(i))
            for hs in range(2):
                cols = slice(hs * DH, (hs + 1) * DH)
                q = qb[p][mine, cols]
                scores = [contract_last(q, kb[p][:, :, cols].reshape(TILE, DH))]
                values = [vb[p][:, :, cols].reshape(TILE, DH)]
                for d in range(1, S):
                    used = count_of(2 * p + hs, tile, lax.rem(tile + S - d, S)) * BLOCK
                    live = lane < used if hs == 0 else lane >= width - used
                    bias = jnp.where(live, 0.0, -jnp.inf).astype(jnp.float32)
                    far = fk[p, d - 1, 0, hs : hs + MOST].reshape(width, DH)
                    scores.append(contract_last(q, far) + bias)
                    values.append(fk[p, d - 1, 1, hs : hs + MOST].reshape(width, DH))
                top = functools.reduce(
                    jnp.maximum, [jnp.max(s, axis=1, keepdims=True) for s in scores]
                )
                total = jnp.zeros((rows, 1), jnp.float32)
                mixed = jnp.zeros((rows, DH), jnp.float32)
                for s, v in zip(scores, values):
                    w = jnp.exp2((s - top) * factor)
                    total = total + jnp.sum(w, axis=1, keepdims=True)
                    mixed = mixed + jnp.dot(
                        w.astype(jnp.bfloat16), v, preferred_element_type=jnp.float32
                    )
                ob[p, i, :, cols] = (mixed / total).astype(jnp.bfloat16)

            @pl.when(i < H - 1)
            def _():
                o_copy(p, i, False).start()

            return carry

        lax.fori_loop(0, H, chunk, 0)
        o_own(p).start()

    for p in range(pairs):
        o_own(p).wait()
        for i in range(H - 1):
            o_copy(p, i32(i), True).wait_recv()
    for d in range(1, S):
        l_copy(d).wait_send()
        for p in range(pairs):
            for c in range(2):
                z_copy(p, d, c).wait_send()
    for p in range(pairs):
        for i in range(H - 1):
            for a in range(3):
                x_copy(a, p, i, False).wait_send()
            o_copy(p, i32(i), False).wait_send()


def on_device(query_rows, key_rows, value_rows, block_lists, block_counts):
    H = lax.axis_size("head")
    S = lax.axis_size("seq")
    me = lax.axis_index("head")
    rows = query_rows.shape[0]
    heads = HEADS // H
    pairs = heads // 2
    mine = lax.dynamic_slice_in_dim(block_lists[:, 0], me * heads, heads)
    tile = lax.axis_index("seq")
    counts = lax.dynamic_slice(block_counts, (me * heads, tile, 0), (heads, 1, S))
    lists = jnp.concatenate(
        [jnp.transpose(mine, (1, 0, 2)).reshape(S, heads * MOST), jnp.transpose(counts[:, 0])],
        axis=1,
    )
    lists = jnp.pad(lists, ((0, 0), (0, 128 - heads * (MOST + 1))))[:, None]
    bf16 = jnp.bfloat16
    piece = math.gcd(rows, BLOCK)
    pieces = (rows // piece, piece, query_rows.shape[1])
    tile_buffers = [
        pltpu.VMEM((TILE // piece, piece, 2 * DH), bf16) for _ in range(2 * pairs)
    ] + [pltpu.VMEM((TILE, 2 * DH), bf16) for _ in range(pairs)]
    anywhere = pl.BlockSpec(memory_space=pl.ANY)
    return pl.pallas_call(
        functools.partial(body, (H, S, rows, heads, piece)),
        out_shape=jax.ShapeDtypeStruct(query_rows.shape, bf16),
        in_specs=[anywhere] * 4,
        out_specs=anywhere,
        scratch_shapes=tile_buffers
        + [
            pltpu.VMEM((pairs, H, rows, 2 * DH), bf16),
            pltpu.VMEM((pairs, S - 1, 2, PAIR_MOST, BLOCK, DH), bf16),
            pltpu.VMEM((pairs, S - 1, 2, PAIR_MOST, BLOCK, DH), bf16),
            pltpu.VMEM((S - 1, 1, 128), jnp.int32),
            pltpu.SMEM((S - 1, 1, 128), jnp.int32),
            pltpu.SMEM((S, 1, 128), jnp.int32),
            pltpu.SemaphoreType.DMA((3, pairs, H)),
            pltpu.SemaphoreType.DMA((3, pairs, H)),
            pltpu.SemaphoreType.DMA((pairs, S - 1, 2)),
            pltpu.SemaphoreType.DMA((pairs, S - 1, 2)),
            pltpu.SemaphoreType.DMA((S - 1,)),
            pltpu.SemaphoreType.DMA((S - 1,)),
            pltpu.SemaphoreType.DMA((2,)),
            pltpu.SemaphoreType.DMA((pairs, H)),
            pltpu.SemaphoreType.DMA((pairs, H)),
        ],
        compiler_params=pltpu.CompilerParams(
            collective_id=0, has_side_effects=True, vmem_limit_bytes=60 << 20
        ),
        name="block_attention",
    )(lists, query_rows, key_rows.reshape(pieces), value_rows.reshape(pieces))


def solution(mesh):
    in_specs = (
        P(("parts", "seq", "head"), None),
        P(("parts", "seq", "head"), None),
        P(("parts", "seq", "head"), None),
        P("parts", "seq", None, None),
        P("parts", None, None),
    )
    out_specs = P(("parts", "seq", "head"), None)
    return jax.shard_map(
        on_device, mesh=mesh, in_specs=in_specs, out_specs=out_specs, check_vma=False
    )
```
